32 devices in a mesh: groups: 2 (over y), ctx: 4 (over z), dom: 2 (over x), tp: 2 (over core).
Axes of the slice: x: 2, y: 2, z: 4, core: 2. Of those that a mesh axis runs over, the one named last changes fastest.
Arguments:
- queries: bfloat16 [8, 32, 8, 8, 128], P('groups', 'dom', 'tp'), parts along dimension 0, may hold values from -8 to 8
- prompt_cache: bfloat16 [4, 8192, 8, 128], P('groups', 'ctx', 'tp'), parts along dimension 0, may hold values from -8 to 8
- suffix_cache: bfloat16 [4, 32, 16, 8, 128], P('groups', 'dom', 'ctx', 'tp'), parts along dimension 0, may hold values from -8 to 8
- new_kv: bfloat16 [8, 2, 32, 8, 128], P('groups', None, 'dom', 'tp'), parts along dimension 0, may hold values from -8 to 8
- ancestors: int32 [8, 32], P('groups'), parts along dimension 0, may hold values from 0 to 31, as said below
- lengths: int32 [64], P('groups'), parts along dimension 0, may hold values from 1 to 12, as said below
Outputs:
- attended: bfloat16 [8, 32, 8, 8, 128], P('groups', 'dom', 'tp'), parts along dimension 0
The draws below stay inside these ranges and needn't reach their ends.
There are 2 independent parts, one for each index of `groups`. The reference program is written for one: setup_inputs(seed, part) draws one part's arguments, and reference() takes and returns one part's arrays. A program takes and returns all parts, laid end to end along the dimension named above; each array names one. Nothing has to cross between parts.
Inputs may be any that keep to these rules, and one draw needn't show every extreme that they name: `ancestors`: particle p is owned by owner p // 16. In every step, of the 16 offspring of one owner at most 16 have their ancestor among the particles of any one owner, and each owner has exactly 16 from some one owner. `lengths`: the largest length is reached in every draw.
All inputs are finite; a program needn't handle non-finite values.
Results may differ from the reference program's by a relative error of at most 0.005.
Values may be sent and summed in bfloat16 or wider, within the bound.
A program may use at most 128 MiB of HBM per device.

```python
import math
import jax
import jax.numpy as jnp
from jax import lax

KVH = 8
GROUP = 8
HD = 128
PART_DEV = 16
STEPS = 4
OWNERS = 2
PARTICLES = 32
PROMPT = 8192
SUF = 16
CAP = 16


def shared_dirs(key):
    base_key = jax.random.fold_in(key, 977)
    along_key = jax.random.fold_in(base_key, 0)
    suffix_dir = (jax.random.randint(along_key, (KVH, HD), 0, 2) * 2 - 1).astype(jnp.float32)
    return suffix_dir


def suffix_shift():
    mass_ratio = max(math.log(PROMPT / SUF), 1.0)
    return math.sqrt(mass_ratio / (math.sqrt(HD) + 2.0))


def drawn_noise(noise_key, full_shape):
    return jnp.clip(jax.random.normal(noise_key, full_shape, jnp.float32), -6.0, 6.0)


def draw_queries(key, part):
    suffix_dir = shared_dirs(key)
    shift_size = suffix_shift()
    noise_key = jax.random.fold_in(jax.random.fold_in(key, 1), 0)
    full_shape = (STEPS, PARTICLES, KVH, GROUP, HD)
    direction = suffix_dir[None, None, :, None, :]
    values = 2.0 * drawn_noise(noise_key, full_shape) + shift_size * direction
    return jnp.clip(values, -8.0, 8.0).astype(jnp.bfloat16)


def draw_prompt_cache(key, part):
    noise_key = jax.random.fold_in(jax.random.fold_in(key, 2), 0)
    full_shape = (2, PROMPT, KVH, HD)
    values = drawn_noise(noise_key, full_shape)
    return jnp.clip(values, -8.0, 8.0).astype(jnp.bfloat16)


def draw_suffix_cache(key, part):
    suffix_dir = shared_dirs(key)
    shift_size = suffix_shift()
    noise_key = jax.random.fold_in(jax.random.fold_in(key, 3), 0)
    full_shape = (2, PARTICLES, SUF, KVH, HD)
    noise_part = drawn_noise(noise_key, full_shape)
    key_rows = noise_part[0] + shift_size * suffix_dir[None, None]
    values = jnp.stack([key_rows, noise_part[1]])
    return jnp.clip(values, -8.0, 8.0).astype(jnp.bfloat16)


def draw_new_kv(key, part):
    suffix_dir = shared_dirs(key)
    shift_size = suffix_shift()
    noise_key = jax.random.fold_in(jax.random.fold_in(key, 4), 0)
    full_shape = (STEPS, 2, PARTICLES, KVH, HD)
    noise_part = drawn_noise(noise_key, full_shape)
    key_rows = noise_part[:, 0] + shift_size * suffix_dir[None, None]
    values = jnp.stack([key_rows, noise_part[:, 1]], axis=1)
    return jnp.clip(values, -8.0, 8.0).astype(jnp.bfloat16)


def draw_lengths(key, part):
    value_key, pick_key = jax.random.split(jax.random.fold_in(key, 5))
    values = jax.random.randint(value_key, (PARTICLES,), 1, SUF - STEPS + 1)
    chosen = jax.random.randint(pick_key, (), 0, PARTICLES)
    return jnp.where(jnp.arange(PARTICLES) == chosen, SUF - STEPS, values).astype(jnp.int32)


def draw_ancestors(key, part):

    def one_owner(owner_key):
        first_key, other_key, order_key, local_key = jax.random.split(owner_key, 4)
        first_source = jax.random.randint(first_key, (), 0, OWNERS)
        others = (first_source + 1 + jnp.arange((OWNERS - 1) * CAP) // CAP) % OWNERS
        others = jax.random.permutation(other_key, others)[:PART_DEV - CAP]
        sources = jnp.concatenate([jnp.full((CAP,), first_source, jnp.int32), others.astype(jnp.int32)])
        sources = jax.random.permutation(order_key, sources)
        local_index = jax.random.randint(local_key, (PART_DEV,), 0, PART_DEV)
        return (sources * PART_DEV + local_index).astype(jnp.int32)

    def one_step(step_key):
        return jax.vmap(one_owner)(jax.random.split(step_key, OWNERS)).reshape(PARTICLES)
    return jax.vmap(one_step)(jax.random.split(jax.random.fold_in(key, 6), STEPS))


def setup_inputs(seed: int = 0, part: int = 0) -> dict:
    arg_keys = jax.random.split(jax.random.key(seed), 7)
    part_splits = jax.random.split(jax.random.fold_in(arg_keys[6], part), 7)
    return {
        "queries": draw_queries(jax.random.fold_in(jax.random.fold_in(arg_keys[6], part), 71), part),
        "prompt_cache": draw_prompt_cache(jax.random.fold_in(jax.random.fold_in(arg_keys[6], part), 71), part),
        "suffix_cache": draw_suffix_cache(jax.random.fold_in(jax.random.fold_in(arg_keys[6], part), 71), part),
        "new_kv": draw_new_kv(jax.random.fold_in(jax.random.fold_in(arg_keys[6], part), 71), part),
        "ancestors": draw_ancestors(jax.random.fold_in(jax.random.fold_in(arg_keys[6], part), 71), part),
        "lengths": draw_lengths(jax.random.fold_in(jax.random.fold_in(arg_keys[6], part), 71), part),
    }


def attend(query_block, prompt_cache, suffix_rows, visible, score_scale):
    operands = (jnp.moveaxis(query_block, 1, 0), jnp.moveaxis(prompt_cache[0], 1, 0), jnp.moveaxis(prompt_cache[1], 1, 0), jnp.moveaxis(suffix_rows[0], 2, 0), jnp.moveaxis(suffix_rows[1], 2, 0))

    def one_head(pieces):
        query_head, prompt_keys, prompt_values, suffix_keys, suffix_values = pieces
        query_wide = query_head.astype(jnp.float32)
        prompt_scores = jnp.einsum('pgd,td->pgt', query_wide, prompt_keys.astype(jnp.float32)) * score_scale
        suffix_scores = jnp.einsum('pgd,psd->pgs', query_wide, suffix_keys.astype(jnp.float32)) * score_scale
        suffix_scores = jnp.where(visible[:, None, :], suffix_scores, -jnp.inf)
        peak_score = jnp.maximum(lax.optimization_barrier(jnp.max(prompt_scores, axis=-1)), lax.optimization_barrier(jnp.max(suffix_scores, axis=-1)))
        prompt_exp = jnp.exp(prompt_scores - peak_score[..., None])
        suffix_exp = jnp.exp(suffix_scores - peak_score[..., None])
        totals = lax.optimization_barrier(jnp.sum(prompt_exp, axis=-1)) + lax.optimization_barrier(jnp.sum(suffix_exp, axis=-1))
        prompt_weights = lax.optimization_barrier(prompt_exp.astype(jnp.bfloat16)).astype(jnp.float32)
        suffix_weights = lax.optimization_barrier(suffix_exp.astype(jnp.bfloat16)).astype(jnp.float32)
        numerator = jnp.einsum('pgt,td->pgd', prompt_weights, prompt_values.astype(jnp.float32))
        numerator = numerator + jnp.einsum('pgs,psd->pgd', suffix_weights, suffix_values.astype(jnp.float32))
        return (numerator / totals[..., None]).astype(jnp.bfloat16)
    per_head = lax.map(one_head, operands)
    return jnp.moveaxis(per_head, 0, 1)

def reference(queries, prompt_cache, suffix_cache, new_kv, ancestors, lengths):
    score_scale = 1.0 / math.sqrt(HD)
    suffix_rows = suffix_cache
    lengths_now = lengths
    positions = jnp.arange(SUF).astype(jnp.int32)
    results = []
    for step_index in range(STEPS):
        parents = ancestors[step_index]
        suffix_rows = jnp.take(suffix_rows, parents, axis=1)
        lengths_now = jnp.take(lengths_now, parents)
        new_slot = positions[None, :] == lengths_now[:, None]
        suffix_rows = jnp.where(new_slot[None, :, :, None, None], new_kv[step_index][:, :, None], suffix_rows)
        visible = positions[None, :] <= lengths_now[:, None]
        results.append(attend(queries[step_index], prompt_cache, suffix_rows, visible, score_scale))
        lengths_now = lengths_now + 1
    return jnp.stack(results)
```

```python
import functools
import math

import jax
import jax.numpy as jnp
from jax import lax
from jax.experimental import pallas as pl
from jax.experimental.pallas import tpu as pltpu
from jax.sharding import PartitionSpec as P

MESH = pl.DeviceIdType.MESH
SG = 2
CS = 2
AHEAD = 2
D_FOLD, D_SWAP = 2, 5
F32, BF16 = jnp.float32, jnp.bfloat16


def log2_int(n):
    assert n & (n - 1) == 0
    return n.bit_length() - 1


def nt(a, b):
    return lax.dot_general(a, b, (((1,), (1,)), ((), ())), preferred_element_type=F32)


def nn(a, b):
    return jnp.dot(a, b, preferred_element_type=F32)


def iota(shape, dim):
    return lax.broadcasted_iota(jnp.int32, shape, dim)


def kernel(
    n_ctx, owners, suf_dev, score_mul,
    q_hbm, prompt_hbm, suf_hbm, new_hbm, anc_hbm, len_hbm, out_ref,
    q_ref, anc_ref, len_ref,
    raw, kf, vf, kh, vth, kx, vx, s_scr,
    suf_g, new_g, sfk, sfv, nfk, nfv, mask,
    acc, stat, msg, got_out, got_in, gst_out, gst_in, fin,
    load_sem, small_sem, ex_local, ex_send, ex_recv,
    rs_send, rs_recv_out, rs_recv_in, ag_send, ag_recv,
):
    steps, per, heads, group, hd = q_ref.shape
    particles = per * owners
    prompt = kh.shape[0]
    rows = SG * per * group
    groups_of_steps = steps // SG
    nb = heads * groups_of_steps
    cuts = SG // CS
    width = CS * per * group
    lo, hi = n_ctx // 2 - 1, n_ctx // 2
    z = lax.axis_index("ctx")
    me = lax.axis_index("dom")
    n_suf = particles * suf_dev
    shares = n_ctx // steps
    chunk = per // shares
    n_new = owners * chunk
    n_ext = mask.shape[1]
    my_step = z // shares
    p0 = lax.rem(z, shares) * chunk

    loads = [
        pltpu.make_async_copy(prompt_hbm.at[i], raw.at[i], load_sem.at[i]) for i in range(2)
    ]
    small = [
        pltpu.make_async_copy(src, dst, small_sem.at[i])
        for i, (src, dst) in enumerate(((anc_hbm, anc_ref), (len_hbm, len_ref), (q_hbm, q_ref)))
    ]
    for c in small[:2] + loads + small[2:]:
        c.start()

    barrier = pltpu.get_barrier_semaphore()
    for d in range(1, owners):
        pl.semaphore_signal(
            barrier, inc=1, device_id={"dom": lax.rem(me + d, owners)}, device_id_type=MESH
        )

    @pl.when(z > 0)
    def _():
        pl.semaphore_signal(barrier, inc=1, device_id={"ctx": z - 1}, device_id_type=MESH)

    @pl.when(z < n_ctx - 1)
    def _():
        pl.semaphore_signal(barrier, inc=1, device_id={"ctx": z + 1}, device_id_type=MESH)

    expected = (owners - 1) + jnp.where(z > 0, 1, 0) + jnp.where(z < n_ctx - 1, 1, 0)
    pl.semaphore_wait(barrier, expected)

    if shares == 1:
        new_src = new_hbm.at[my_step]
    else:
        new_src = new_hbm.at[
            my_step, :, pl.ds(pl.multiple_of(p0 * heads, chunk * heads), chunk * heads), :
        ]
    exchange = []
    for d in range(1, owners):
        peer = {"dom": lax.rem(me + d, owners)}
        for i, (src, dst) in enumerate(((suf_hbm, suf_g), (new_src, new_g))):
            exchange.append(
                pltpu.make_async_remote_copy(
                    src_ref=src, dst_ref=dst.at[me],
                    send_sem=ex_send.at[i, d - 1], recv_sem=ex_recv.at[i, d - 1],
                    device_id=peer, device_id_type=MESH,
                )
            )
    own = [
        pltpu.make_async_copy(suf_hbm, suf_g.at[me], ex_local.at[0]),
        pltpu.make_async_copy(new_src, new_g.at[me], ex_local.at[1]),
    ]
    for c in exchange + own:
        c.start()

    for c in small[:2]:
        c.wait()
    key = iota((n_ext, particles), 0)
    col = iota((n_ext, particles), 1)
    suf_particle = key >> log2_int(suf_dev)
    suf_pos = (key & (suf_dev - 1)) + z * suf_dev
    reach = (key < n_suf) & (suf_particle == col) & (suf_pos < len_ref[...])
    state = jnp.where(reach, 1.0, 0.0)
    rest = key - n_suf
    new_particle = (rest >> log2_int(chunk)) * per + (rest & (chunk - 1)) + p0
    is_new = jnp.where(
        (rest >= 0) & (rest < n_new) & (new_particle == col), 1.0, 0.0
    )
    spread = jnp.where(
        iota((particles, per * group), 0)
        == (iota((particles, per * group), 1) >> log2_int(group)) + me * per,
        1.0, 0.0,
    ).astype(BF16)
    for s in range(steps):
        parents = anc_ref[pl.ds(s, 1), :]
        move = jnp.where(iota((particles, particles), 0) == parents, 1.0, 0.0).astype(BF16)
        state = nn(state.astype(BF16), move)
        state = state + is_new * jnp.where(my_step == s, 1.0, 0.0)
        wide = nn(state.astype(BF16), spread)
        mask[s] = jnp.where(wide > 0.5, 0.0, -1e30)

    for src, dst in ((0, kf), (1, vf)):
        loads[src].wait()
        size = 1024

        def widen(i, _, src=src, dst=dst):
            at = pl.ds(pl.multiple_of(i * size, size), size)
            dst[at, :] = raw[src, at, :].astype(F32)
            return 0

        lax.fori_loop(0, raw.shape[1] // size, widen, 0)

    small[2].wait()

    def parts(b):
        h = b // groups_of_steps
        return h, (b - h * groups_of_steps) * SG

    def queries_of(b):
        h, s0 = parts(b)
        out = [
            q_ref[s0 + i, :, h].astype(F32).reshape(per * group, hd) for i in range(SG)
        ]
        return jnp.concatenate(out, axis=0).astype(BF16)

    def extra_rows(suf, new, h):
        pieces = [suf[pl.ds(h, n_suf, stride=heads), :], new[pl.ds(h, n_new, stride=heads), :]]
        if n_ext > n_suf + n_new:
            pieces.append(jnp.zeros((n_ext - n_suf - n_new, hd), F32))
        return jnp.concatenate(pieces, axis=0)

    def bias_of(s0):
        return jnp.concatenate([mask[s0 + i] for i in range(SG)], axis=1)

    def prompt_stage(b, extra):
        h, s0 = parts(b)

        @pl.when(s0 == 0)
        def _():
            size = 256
            for i in range(prompt // size):
                at = pl.ds(h + i * size * heads, size, stride=heads)
                kh[pl.ds(i * size, size), :] = kf[at, :].astype(BF16)
                vth[:, pl.ds(i * size, size)] = vf[at, :].T.astype(BF16)
            if extra:
                kx[...] = extra_rows(sfk, nfk, h).astype(BF16)
                vx[...] = extra_rows(sfv, nfv, h).T.astype(BF16)

        q = queries_of(b)
        size = 512
        top = None
        if extra:
            sx = nt(kx[...], q) * score_mul + bias_of(s0)
        for i in range(prompt // size):
            at = pl.ds(i * size, size)
            s = nt(kh[at, :], q)
            s_scr[at, :] = s
            t = jnp.max(s, axis=0, keepdims=True)
            top = t if top is None else jnp.maximum(top, t)
        top = top * score_mul
        total = jnp.zeros((1, rows), F32)
        numer = jnp.zeros((hd, rows), F32)
        if extra:
            top = jnp.maximum(top, jnp.max(sx, axis=0, keepdims=True))
            w = jnp.exp2(sx - top)
            total += jnp.sum(w, axis=0, keepdims=True)
            numer += nn(vx[...], w.astype(BF16))
        for i in range(prompt // size):
            at = pl.ds(i * size, size)
            w = jnp.exp2(s_scr[at, :] * score_mul - top)
            total += jnp.sum(w, axis=0, keepdims=True)
            numer += nn(vth[:, at], w.astype(BF16))
        put(b, top, total, numer, extra)
        if extra:
            start_inward(b)

    def put(b, top, total, numer, ready):
        small = jnp.where(iota((2, rows), 0) == 0, top, total)
        for i in range(cuts):
            at = slice(i * width, (i + 1) * width)
            stat[b * cuts + i] = small[:, at]
            acc[b * cuts + i] = numer[:, at]
            if ready:
                msg[b * cuts + i] = numer[:, at].astype(BF16)

    def unpack_extra():
        for c in own:
            c.wait()
        for c in exchange:
            c.wait()
        ps, pn = suf_g.shape[2], new_g.shape[2]
        for o in range(owners):
            for i, dst in enumerate((sfk, sfv)):
                dst[pl.ds(o * ps, ps), :] = suf_g[o, i].astype(F32)
            for i, dst in enumerate((nfk, nfv)):
                dst[pl.ds(o * pn, pn), :] = new_g[o, i].astype(F32)

    def local_stage(b):
        h, s0 = parts(b)
        ks = extra_rows(sfk, nfk, h).astype(BF16)
        vt = extra_rows(sfv, nfv, h).T.astype(BF16)
        s = nt(ks, queries_of(b)) * score_mul + bias_of(s0)
        small = jnp.concatenate([stat[b * cuts + i] for i in range(cuts)], axis=1)
        old_numer = jnp.concatenate([acc[b * cuts + i] for i in range(cuts)], axis=1)
        old_top, old_total = small[0:1], small[1:2]
        new_top = jnp.maximum(old_top, jnp.max(s, axis=0, keepdims=True))
        w = jnp.exp2(s - new_top)
        keep = jnp.exp2(old_top - new_top)
        total = old_total * keep + jnp.sum(w, axis=0, keepdims=True)
        numer = old_numer * keep + nn(vt, w.astype(BF16))
        put(b, new_top, total, numer, True)
        start_inward(b)

    mid = (z == lo) | (z == hi)
    left_half = z <= lo
    inner = jnp.where(left_half, z + 1, z - 1)
    outer = jnp.where(left_half, z - 1, z + 1)
    has_outer = (z > 0) & (z < n_ctx - 1)

    def inward(c, across):
        data, small, sems = (
            (got_in, gst_in, rs_recv_in) if across else (got_out, gst_out, rs_recv_out)
        )
        return [
            pltpu.make_async_remote_copy(
                src_ref=src.at[c], dst_ref=dst.at[c],
                send_sem=rs_send.at[i, c], recv_sem=sems.at[i, c],
                device_id={"ctx": inner}, device_id_type=MESH,
            )
            for i, (src, dst) in enumerate(((stat, small), (msg, data)))
        ]

    def outward(c):
        return pltpu.make_async_remote_copy(
            src_ref=fin.at[c], dst_ref=fin.at[c],
            send_sem=ag_send.at[c], recv_sem=ag_recv.at[c],
            device_id={"ctx": outer}, device_id_type=MESH,
        )

    def start_inward(b):
        @pl.when(jnp.logical_not(has_outer))
        def _():
            for i in range(cuts):
                send(b * cuts + i)

    def send(c):
        for across in (True, False):
            @pl.when(mid if across else jnp.logical_not(mid))
            def _(across=across):
                for copy in inward(c, across):
                    copy.start()

    def merge(first, second):
        m1, l1, a1 = first
        m2, l2, a2 = second
        m = jnp.maximum(m1, m2)
        c1, c2 = jnp.exp2(m1 - m), jnp.exp2(m2 - m)
        return m, l1 * c1 + l2 * c2, a1 * c1 + a2 * c2

    def fold_stage(c):
        @pl.when(has_outer)
        def _():
            for copy in inward(c, False):
                copy.wait_recv()
            top, total, numer = merge(
                (stat[c, 0:1, :], stat[c, 1:2, :], acc[c]),
                (gst_out[c, 0:1, :], gst_out[c, 1:2, :], got_out[c].astype(F32)),
            )
            stat[c] = jnp.where(iota((2, width), 0) == 0, top, total)
            msg[c] = numer.astype(BF16)
            send(c)

    def put_out(c):
        h = c // (groups_of_steps * cuts)
        s0 = (c - h * (groups_of_steps * cuts)) * CS
        for i in range(CS):
            out_ref[s0 + i, :, h] = fin[c, i]

    def swap_stage(c):
        @pl.when(mid)
        def _():
            for copy in inward(c, True):
                copy.wait_recv()
            mine = (stat[c], msg[c].astype(F32))
            theirs = (gst_in[c], got_in[c].astype(F32))
            low = [jnp.where(left_half, a, b) for a, b in zip(mine, theirs)]
            high = [jnp.where(left_half, b, a) for a, b in zip(mine, theirs)]
            _, total, numer = merge(
                (low[0][0:1], low[0][1:2], low[1]), (high[0][0:1], high[0][1:2], high[1])
            )
            done = numer / total
            for i in range(CS):
                wide = done[:, i * per * group:(i + 1) * per * group].T
                fin[c, i] = wide.reshape(per, group, hd).astype(BF16)

            @pl.when(has_outer)
            def _():
                outward(c).start()

            put_out(c)

    def spread_stage(c):
        @pl.when(jnp.logical_not(mid))
        def _():
            outward(c).wait_recv()

            @pl.when(has_outer)
            def _():
                outward(c).start()

            put_out(c)

        for across in (True, False):
            @pl.when(mid if across else jnp.logical_not(mid))
            def _(across=across):
                for copy in inward(c, across):
                    copy.wait_send()

        @pl.when(has_outer)
        def _():
            outward(c).wait_send()

    def each(stage, b):
        for i in range(cuts):
            stage(b * cuts + i)

    def run(i, _):
        @pl.when(i < AHEAD)
        def _():
            prompt_stage(i, False)

        @pl.when(i == AHEAD)
        def _():
            unpack_extra()

            def add(b, _):
                local_stage(b)
                return 0

            lax.fori_loop(0, AHEAD, add, 0)

        @pl.when((i >= AHEAD) & (i < nb))
        def _():
            prompt_stage(i, True)

        for delay, stage in ((D_FOLD, fold_stage), (D_SWAP, swap_stage)):
            @pl.when((i >= delay) & (i < nb + delay))
            def _(delay=delay, stage=stage):
                each(stage, i - delay)
        return 0

    lax.fori_loop(0, nb + D_SWAP, run, 0)

    def close(c, _):
        spread_stage(c)
        return 0

    lax.fori_loop(0, nb * cuts, close, 0)


def on_device(n_ctx, owners, queries, prompt_cache, suffix_cache, new_kv, ancestors, lengths):
    steps, per, heads, group, hd = queries.shape
    prompt = prompt_cache.shape[1]
    suf_dev = suffix_cache.shape[2]
    particles = ancestors.shape[1]
    rows = SG * per * group
    nc = heads * (steps // CS)
    width = CS * per * group
    shares = n_ctx // steps
    chunk = per // shares
    n_ext = -(-(particles * suf_dev + owners * chunk) // 128) * 128
    dma = pltpu.SemaphoreType.DMA
    score_mul = math.log2(math.e) / math.sqrt(hd)
    ps, pn = per * suf_dev * heads, chunk * heads
    any_spec = pl.BlockSpec(memory_space=pl.ANY)
    vmem_spec = pl.BlockSpec(memory_space=pltpu.VMEM)
    return pl.pallas_call(
        functools.partial(kernel, n_ctx, owners, suf_dev, score_mul),
        out_shape=pltpu.VMEM(queries.shape, BF16),
        in_specs=[any_spec] * 6,
        out_specs=vmem_spec,
        scratch_shapes=[
            pltpu.VMEM(queries.shape, BF16),
            pltpu.VMEM(ancestors.shape, jnp.int32),
            pltpu.VMEM((1, particles), jnp.int32),
            pltpu.VMEM((2, prompt * heads, hd), BF16),
            pltpu.VMEM((prompt * heads, hd), F32),
            pltpu.VMEM((prompt * heads, hd), F32),
            pltpu.VMEM((prompt, hd), BF16),
            pltpu.VMEM((hd, prompt), BF16),
            pltpu.VMEM((n_ext, hd), BF16),
            pltpu.VMEM((hd, n_ext), BF16),
            pltpu.VMEM((prompt, rows), F32),
            pltpu.VMEM((owners, 2, ps, hd), BF16),
            pltpu.VMEM((owners, 2, pn, hd), BF16),
            pltpu.VMEM((owners * ps, hd), F32),
            pltpu.VMEM((owners * ps, hd), F32),
            pltpu.VMEM((owners * pn, hd), F32),
            pltpu.VMEM((owners * pn, hd), F32),
            pltpu.VMEM((steps, n_ext, per * group), F32),
            pltpu.VMEM((nc, hd, width), F32),
            pltpu.VMEM((nc, 2, width), F32),
            pltpu.VMEM((nc, hd, width), BF16),
            pltpu.VMEM((nc, hd, width), BF16),
            pltpu.VMEM((nc, hd, width), BF16),
            pltpu.VMEM((nc, 2, width), F32),
            pltpu.VMEM((nc, 2, width), F32),
            pltpu.VMEM((nc, CS, per, group, hd), BF16),
            dma((2,)),
            dma((3,)),
            dma((2,)),
            dma((2, max(owners - 1, 1))),
            dma((2, max(owners - 1, 1))),
            dma((2, nc)),
            dma((2, nc)),
            dma((2, nc)),
            dma((nc,)),
            dma((nc,)),
        ],
        compiler_params=pltpu.CompilerParams(
            collective_id=0, has_side_effects=True, vmem_limit_bytes=58 << 20
        ),
    )(
        queries,
        prompt_cache.reshape(2, prompt * heads, hd),
        suffix_cache.reshape(2, ps, hd),
        new_kv.reshape(steps, 2, per * heads, hd),
        ancestors,
        lengths.reshape(1, particles),
    )


def solution(mesh):
    return jax.shard_map(
        functools.partial(on_device, mesh.shape["ctx"], mesh.shape["dom"]),
        mesh=mesh,
        in_specs=(
            P("groups", "dom", "tp", None, None),
            P("groups", "ctx", "tp", None),
            P("groups", "dom", "ctx", "tp", None),
            P("groups", None, "dom", "tp", None),
            P("groups", None),
            P("groups"),
        ),
        out_specs=P("groups", "dom", "tp", None, None),
        check_vma=False,
    )
```

```python
import functools
import math

import jax
import jax.numpy as jnp
from jax import lax
from jax.experimental import pallas as pl
from jax.experimental.pallas import tpu as pltpu
from jax.sharding import PartitionSpec as P

MESH = pl.DeviceIdType.MESH
SG = 2
PIECES = 4
TILE = 256
FOLD_LEFT, FOLD_RIGHT = 2, 2
SWAP_LEFT, SWAP_RIGHT = 5, 2
MASKED = -1e30
F32, BF16 = jnp.float32, jnp.bfloat16


def log2_int(n):
    assert n & (n - 1) == 0
    return n.bit_length() - 1


def nt(a, b):
    return lax.dot_general(a, b, (((1,), (1,)), ((), ())), preferred_element_type=F32)


def nn(a, b):
    return jnp.dot(a, b, preferred_element_type=F32)


def iota(shape, dim):
    return lax.broadcasted_iota(jnp.int32, shape, dim)


def kernel(
    n_ctx, owners, suf_dev, score_mul,
    q_hbm, prompt_hbm, suf_hbm, new_hbm, anc_hbm, len_hbm, out_ref,
    q_ref, anc_ref, len_ref, raw, kf, vf, kx, vx, s_scr, lse_scr,
    suf_g, new_g, sfk, sfv, nfk, nfv, mask,
    own, stat, msg, got_out, got_in, gst_out, gst_in,
    load_sem, small_sem, ex_local, ex_send, ex_recv,
    rs_send, rs_recv_out, rs_recv_in, ag_send, ag_recv,
):
    steps, per, heads, group, hd = q_ref.shape
    particles = per * owners
    prompt = kf.shape[0] // heads
    width = per * group
    rows = SG * width
    groups_of_steps = steps // SG
    nb = heads * groups_of_steps
    lo, hi = n_ctx // 2 - 1, n_ctx // 2
    z = lax.axis_index("ctx")
    me = lax.axis_index("dom")
    n_suf = particles * suf_dev
    shares = n_ctx // steps
    chunk = per // shares
    n_new = owners * chunk
    n_ext = mask.shape[2]
    my_step = z // shares
    p0 = lax.rem(z, shares) * chunk

    barrier = pltpu.get_barrier_semaphore()
    for d in range(1, owners):
        pl.semaphore_signal(
            barrier, inc=1, device_id={"dom": lax.rem(me + d, owners)}, device_id_type=MESH
        )

    @pl.when(z > 0)
    def _():
        pl.semaphore_signal(barrier, inc=1, device_id={"ctx": z - 1}, device_id_type=MESH)

    @pl.when(z < n_ctx - 1)
    def _():
        pl.semaphore_signal(barrier, inc=1, device_id={"ctx": z + 1}, device_id_type=MESH)

    piece = raw.shape[1] // PIECES
    loads = [
        [
            pltpu.make_async_copy(
                prompt_hbm.at[i, pl.ds(j * piece, piece)],
                raw.at[i, pl.ds(j * piece, piece)],
                load_sem.at[i, j],
            )
            for j in range(PIECES)
        ]
        for i in range(2)
    ]
    small = [
        pltpu.make_async_copy(src, dst, small_sem.at[i])
        for i, (src, dst) in enumerate(((anc_hbm, anc_ref), (len_hbm, len_ref), (q_hbm, q_ref)))
    ]
    for c in small[:2] + loads[0] + small[2:] + loads[1]:
        c.start()

    expected = (owners - 1) + jnp.where(z > 0, 1, 0) + jnp.where(z < n_ctx - 1, 1, 0)
    pl.semaphore_wait(barrier, expected)

    if shares == 1:
        new_src = new_hbm.at[my_step]
    else:
        new_src = new_hbm.at[
            my_step, :, pl.ds(pl.multiple_of(p0 * heads, chunk * heads), chunk * heads), :
        ]
    exchange = []
    for d in range(1, owners):
        peer = {"dom": lax.rem(me + d, owners)}
        for i, (src, dst) in enumerate(((suf_hbm, suf_g), (new_src, new_g))):
            exchange.append(
                pltpu.make_async_remote_copy(
                    src_ref=src, dst_ref=dst.at[me],
                    send_sem=ex_send.at[i, d - 1], recv_sem=ex_recv.at[i, d - 1],
                    device_id=peer, device_id_type=MESH,
                )
            )
    local = [
        pltpu.make_async_copy(suf_hbm, suf_g.at[me], ex_local.at[0]),
        pltpu.make_async_copy(new_src, new_g.at[me], ex_local.at[1]),
    ]
    for c in exchange + local:
        c.start()

    for c in small[:2]:
        c.wait()
    key = iota((n_ext, particles), 0)
    col = iota((n_ext, particles), 1)
    suf_particle = key >> log2_int(suf_dev)
    suf_pos = (key & (suf_dev - 1)) + z * suf_dev
    reach = (key < n_suf) & (suf_particle == col) & (suf_pos < len_ref[...])
    state = jnp.where(reach, 1.0, 0.0)
    rest = key - n_suf
    new_particle = (rest >> log2_int(chunk)) * per + (rest & (chunk - 1)) + p0
    is_new = jnp.where(
        (rest >= 0) & (rest < n_new) & (new_particle == col), 1.0, 0.0
    )
    spread = jnp.where(
        iota((width, particles), 1) == (iota((width, particles), 0) >> log2_int(group)) + me * per,
        1.0, 0.0,
    ).astype(BF16)
    for s in range(steps):
        parents = anc_ref[pl.ds(s, 1), :]
        move = jnp.where(iota((particles, particles), 0) == parents, 1.0, 0.0).astype(BF16)
        state = nn(state.astype(BF16), move)
        state = state + is_new * jnp.where(my_step == s, 1.0, 0.0)
        mask[s] = jnp.where(nt(spread, state.astype(BF16)) > 0.5, 0.0, MASKED)

    size = 1024
    for src, dst in ((0, kf), (1, vf)):
        for j in range(PIECES):
            loads[src][j].wait()

            def widen(i, _, src=src, dst=dst, j=j):
                at = pl.ds(pl.multiple_of(j * piece + i * size, size), size)
                dst[at, :] = raw[src, at, :].astype(F32)
                return 0

            lax.fori_loop(0, piece // size, widen, 0)

    small[2].wait()
    eye = iota((width, width), 0) == iota((width, width), 1)

    def parts(b):
        h = b // groups_of_steps
        return h, (b - h * groups_of_steps) * SG

    def to_lanes(x):
        return jnp.sum(jnp.where(eye, x, 0.0), axis=0, keepdims=True)

    def to_rows(x):
        return jnp.sum(jnp.where(eye, jnp.broadcast_to(x, eye.shape), 0.0), axis=1, keepdims=True)

    def head_tile(ref, h, i):
        return ref[pl.ds(h + i * TILE * heads, TILE, stride=heads), :].astype(BF16)

    def attend(b, use_prompt, use_extra):
        h, s0 = parts(b)
        q = jnp.concatenate(
            [q_ref[s0 + i, :, h].astype(F32).reshape(width, hd) for i in range(SG)], axis=0
        ).astype(BF16)
        tiles = []
        if use_prompt:
            for i in range(prompt // TILE):
                tiles.append((
                    i * TILE, TILE, None,
                    lambda i=i: head_tile(kf, h, i), lambda i=i: head_tile(vf, h, i),
                ))
        if use_extra:
            tiles.append((
                prompt, n_ext,
                lambda: jnp.concatenate([mask[s0 + i] for i in range(SG)], axis=0),
                lambda: kx[h], lambda: vx[h],
            ))
        peak = None
        for at, size, bias, keys, _ in tiles:
            score = nt(q, keys())
            if bias is not None:
                score = score + bias()
            s_scr[:, pl.ds(at, size)] = score
            for i in range(0, size, hd):
                part = score[:, i:i + hd]
                peak = part if peak is None else jnp.maximum(peak, part)
        peak = jnp.max(peak, axis=1, keepdims=True)
        both = None
        for at, size, _, _, values in tiles:
            w = jnp.exp2((s_scr[:, pl.ds(at, size)] - peak) * score_mul).astype(BF16)
            v = values()
            part = nn(w, jnp.concatenate([v, jnp.ones_like(v)], axis=1))
            both = part if both is None else both + part
        total = both[:, hd:]
        return both[:, :hd] / total, peak * score_mul + jnp.log2(total)

    def put(b, out, lse):
        for i in range(SG):
            c = b * SG + i
            at = slice(i * width, (i + 1) * width)
            own[c] = out[at]
            stat[c] = to_lanes(lse[at])

            @pl.when(jnp.logical_not(has_outer))
            def _(c=c, at=at):
                msg[c] = out[at].astype(BF16)
                send(c)

    def weight(first, second):
        top = jnp.maximum(first, second)
        e1, e2 = jnp.exp2(first - top), jnp.exp2(second - top)
        return e1 / (e1 + e2), top + jnp.log2(e1 + e2)

    def unpack_extra():
        for c in local:
            c.wait()
        for c in exchange:
            c.wait()
        ps, pn = suf_g.shape[2], new_g.shape[2]
        for o in range(owners):
            for i, dst in enumerate((sfk, sfv)):
                dst[pl.ds(o * ps, ps), :] = suf_g[o, i].astype(F32)
            for i, dst in enumerate((nfk, nfv)):
                dst[pl.ds(o * pn, pn), :] = new_g[o, i].astype(F32)
        for h in range(heads):
            for suf, new, dst in ((sfk, nfk, kx), (sfv, nfv, vx)):
                pieces = [
                    suf[pl.ds(h, n_suf, stride=heads), :], new[pl.ds(h, n_new, stride=heads), :]
                ]
                if n_ext > n_suf + n_new:
                    pieces.append(jnp.zeros((n_ext - n_suf - n_new, hd), F32))
                dst[h] = jnp.concatenate(pieces, axis=0).astype(BF16)

    mid = (z == lo) | (z == hi)
    left_half = z <= lo
    inner = jnp.where(left_half, z + 1, z - 1)
    outer = jnp.where(left_half, z - 1, z + 1)
    has_outer = (z > 0) & (z < n_ctx - 1)

    def inward(c, across):
        data, small_to, sems = (
            (got_in, gst_in, rs_recv_in) if across else (got_out, gst_out, rs_recv_out)
        )
        return [
            pltpu.make_async_remote_copy(
                src_ref=src.at[c], dst_ref=dst.at[c],
                send_sem=rs_send.at[i, c], recv_sem=sems.at[i, c],
                device_id={"ctx": inner}, device_id_type=MESH,
            )
            for i, (src, dst) in enumerate(((stat, small_to), (msg, data)))
        ]

    def place(c):
        h = c // steps
        return out_ref.at[c - h * steps, :, h]

    def outward(c):
        return pltpu.make_async_remote_copy(
            src_ref=place(c), dst_ref=place(c),
            send_sem=ag_send.at[c], recv_sem=ag_recv.at[c],
            device_id={"ctx": outer}, device_id_type=MESH,
        )

    def send(c):
        for across in (True, False):
            @pl.when(mid if across else jnp.logical_not(mid))
            def _(across=across):
                for copy in inward(c, across):
                    copy.start()

    def fold_stage(c):
        for copy in inward(c, False):
            copy.wait_recv()
        share, lse = weight(stat[c], gst_out[c])
        theirs = got_out[c].astype(F32)
        msg[c] = (theirs + to_rows(share) * (own[c] - theirs)).astype(BF16)
        stat[c] = lse
        send(c)

    def swap_stage(c):
        for copy in inward(c, True):
            copy.wait_recv()
        mine, theirs = (stat[c], msg[c].astype(F32)), (gst_in[c], got_in[c].astype(F32))
        low = [jnp.where(left_half, a, b) for a, b in zip(mine, theirs)]
        high = [jnp.where(left_half, b, a) for a, b in zip(mine, theirs)]
        share, _ = weight(low[0], high[0])
        done = high[1] + to_rows(share) * (low[1] - high[1])
        place(c)[...] = done.reshape(per, group, hd).astype(BF16)

        @pl.when(has_outer)
        def _():
            outward(c).start()

    def each(stage, b):
        for i in range(SG):
            stage(b * SG + i)

    out, lse = attend(0, True, False)
    own[pl.ds(0, SG)] = out.reshape(SG, width, hd)
    lse_scr[...] = lse
    unpack_extra()
    out_x, lse_x = attend(0, False, True)
    share, lse = weight(lse_scr[...], lse_x)
    put(0, out_x + share * (own[pl.ds(0, SG)].reshape(rows, hd) - out_x), lse)

    fold_delay = jnp.where(left_half, FOLD_LEFT, FOLD_RIGHT)
    swap_delay = jnp.where(left_half, SWAP_LEFT, SWAP_RIGHT)

    def run(i, _):
        @pl.when(i < nb)
        def _():
            put(i, *attend(i, True, True))

        for on, delay, stage in ((has_outer, fold_delay, fold_stage), (mid, swap_delay, swap_stage)):
            @pl.when(on & (i >= delay) & (i < nb + delay))
            def _(delay=delay, stage=stage):
                each(stage, i - delay)
        return 0

    lax.fori_loop(1, nb + max(FOLD_LEFT, FOLD_RIGHT, SWAP_LEFT, SWAP_RIGHT), run, 0)

    def close(c, _):
        @pl.when(jnp.logical_not(mid))
        def _():
            outward(c).wait_recv()

            @pl.when(has_outer)
            def _():
                outward(c).start()

        for across in (True, False):
            @pl.when(mid if across else jnp.logical_not(mid))
            def _(across=across):
                for copy in inward(c, across):
                    copy.wait_send()

        @pl.when(has_outer)
        def _():
            outward(c).wait_send()
        return 0

    lax.fori_loop(0, nb * SG, close, 0)


def on_device(n_ctx, owners, queries, prompt_cache, suffix_cache, new_kv, ancestors, lengths):
    steps, per, heads, group, hd = queries.shape
    prompt = prompt_cache.shape[1]
    suf_dev = suffix_cache.shape[2]
    particles = ancestors.shape[1]
    width = per * group
    rows = SG * width
    nc = heads * steps
    shares = n_ctx // steps
    chunk = per // shares
    n_ext = -(-(particles * suf_dev + owners * chunk) // 128) * 128
    dma = pltpu.SemaphoreType.DMA
    score_mul = math.log2(math.e) / math.sqrt(hd)
    ps, pn = per * suf_dev * heads, chunk * heads
    any_spec = pl.BlockSpec(memory_space=pl.ANY)
    vmem_spec = pl.BlockSpec(memory_space=pltpu.VMEM)
    return pl.pallas_call(
        functools.partial(kernel, n_ctx, owners, suf_dev, score_mul),
        out_shape=pltpu.VMEM(queries.shape, BF16),
        in_specs=[any_spec] * 6,
        out_specs=vmem_spec,
        scratch_shapes=[
            pltpu.VMEM(queries.shape, BF16),
            pltpu.VMEM(ancestors.shape, jnp.int32),
            pltpu.VMEM((1, particles), jnp.int32),
            pltpu.VMEM((2, prompt * heads, hd), BF16),
            pltpu.VMEM((prompt * heads, hd), F32),
            pltpu.VMEM((prompt * heads, hd), F32),
            pltpu.VMEM((heads, n_ext, hd), BF16),
            pltpu.VMEM((heads, n_ext, hd), BF16),
            pltpu.VMEM((rows, prompt + n_ext), F32),
            pltpu.VMEM((rows, hd), F32),
            pltpu.VMEM((owners, 2, ps, hd), BF16),
            pltpu.VMEM((owners, 2, pn, hd), BF16),
            pltpu.VMEM((owners * ps, hd), F32),
            pltpu.VMEM((owners * ps, hd), F32),
            pltpu.VMEM((owners * pn, hd), F32),
            pltpu.VMEM((owners * pn, hd), F32),
            pltpu.VMEM((steps, width, n_ext), F32),
            pltpu.VMEM((nc, width, hd), F32),
            pltpu.VMEM((nc, 1, width), F32),
            pltpu.VMEM((nc, width, hd), BF16),
            pltpu.VMEM((nc, width, hd), BF16),
            pltpu.VMEM((nc, width, hd), BF16),
            pltpu.VMEM((nc, 1, width), F32),
            pltpu.VMEM((nc, 1, width), F32),
            dma((2, PIECES)),
            dma((3,)),
            dma((2,)),
            dma((2, max(owners - 1, 1))),
            dma((2, max(owners - 1, 1))),
            dma((2, nc)),
            dma((2, nc)),
            dma((2, nc)),
            dma((nc,)),
            dma((nc,)),
        ],
        compiler_params=pltpu.CompilerParams(
            collective_id=0, has_side_effects=True, vmem_limit_bytes=58 << 20
        ),
    )(
        queries,
        prompt_cache.reshape(2, prompt * heads, hd),
        suffix_cache.reshape(2, ps, hd),
        new_kv.reshape(steps, 2, per * heads, hd),
        ancestors,
        lengths.reshape(1, particles),
    )


def solution(mesh):
    return jax.shard_map(
        functools.partial(on_device, mesh.shape["ctx"], mesh.shape["dom"]),
        mesh=mesh,
        in_specs=(
            P("groups", "dom", "tp", None, None),
            P("groups", "ctx", "tp", None),
            P("groups", "dom", "ctx", "tp", None),
            P("groups", None, "dom", "tp", None),
            P("groups", None),
            P("groups"),
        ),
        out_specs=P("groups", "dom", "tp", None, None),
        check_vma=False,
    )
```

```python
import functools
import math

import jax
import jax.numpy as jnp
from jax import lax
from jax.experimental import pallas as pl
from jax.experimental.pallas import tpu as pltpu
from jax.sharding import PartitionSpec as P

MESH = pl.DeviceIdType.MESH
SG = 2
PIECES = 4
TILE = 256
FOLD_LEFT, FOLD_RIGHT = 2, 2
SWAP_LEFT, SWAP_RIGHT = 5, 2
MASKED = -1e30
F32, BF16 = jnp.float32, jnp.bfloat16


def log2_int(n):
    assert n & (n - 1) == 0
    return n.bit_length() - 1


def nt(a, b):
    return lax.dot_general(a, b, (((1,), (1,)), ((), ())), preferred_element_type=F32)


def nn(a, b):
    return jnp.dot(a, b, preferred_element_type=F32)


def iota(shape, dim):
    return lax.broadcasted_iota(jnp.int32, shape, dim)


def kernel(
    n_ctx, owners, suf_dev, score_mul,
    q_hbm, prompt_hbm, suf_hbm, new_hbm, anc_hbm, len_hbm, out_ref,
    q_ref, anc_ref, len_ref, raw, kf, vf, kx, vx, s_scr, lse_scr, half_scr,
    suf_g, new_g, sfk, sfv, nfk, nfv, mask,
    own, stat, msg, got_out, got_in, gst_out, gst_in,
    load_sem, small_sem, ex_local, ex_send, ex_recv,
    rs_send, rs_recv_out, rs_recv_in, ag_send, ag_recv,
):
    steps, per, heads, group, hd = q_ref.shape
    particles = per * owners
    prompt = kf.shape[0] // heads
    width = per * group
    rows = SG * width
    groups_of_steps = steps // SG
    nb = heads * groups_of_steps
    lo, hi = n_ctx // 2 - 1, n_ctx // 2
    z = lax.axis_index("ctx")
    me = lax.axis_index("dom")
    n_suf = particles * suf_dev
    shares = n_ctx // steps
    chunk = per // shares
    n_new = owners * chunk
    n_ext = mask.shape[2]
    my_step = z // shares
    p0 = lax.rem(z, shares) * chunk

    barrier = pltpu.get_barrier_semaphore()
    for d in range(1, owners):
        pl.semaphore_signal(
            barrier, inc=1, device_id={"dom": lax.rem(me + d, owners)}, device_id_type=MESH
        )

    @pl.when(z > 0)
    def _():
        pl.semaphore_signal(barrier, inc=1, device_id={"ctx": z - 1}, device_id_type=MESH)

    @pl.when(z < n_ctx - 1)
    def _():
        pl.semaphore_signal(barrier, inc=1, device_id={"ctx": z + 1}, device_id_type=MESH)

    piece = raw.shape[1] // PIECES
    loads = [
        [
            pltpu.make_async_copy(
                prompt_hbm.at[i, pl.ds(j * piece, piece)],
                raw.at[i, pl.ds(j * piece, piece)],
                load_sem.at[i, j],
            )
            for j in range(PIECES)
        ]
        for i in range(2)
    ]
    small = [
        pltpu.make_async_copy(src, dst, small_sem.at[i])
        for i, (src, dst) in enumerate(((anc_hbm, anc_ref), (len_hbm, len_ref), (q_hbm, q_ref)))
    ]
    for c in small[:2] + loads[0] + small[2:] + loads[1]:
        c.start()

    expected = (owners - 1) + jnp.where(z > 0, 1, 0) + jnp.where(z < n_ctx - 1, 1, 0)
    pl.semaphore_wait(barrier, expected)

    if shares == 1:
        new_src = new_hbm.at[my_step]
    else:
        new_src = new_hbm.at[
            my_step, :, pl.ds(pl.multiple_of(p0 * heads, chunk * heads), chunk * heads), :
        ]
    exchange = []
    for d in range(1, owners):
        peer = {"dom": lax.rem(me + d, owners)}
        for i, (src, dst) in enumerate(((suf_hbm, suf_g), (new_src, new_g))):
            exchange.append(
                pltpu.make_async_remote_copy(
                    src_ref=src, dst_ref=dst.at[me],
                    send_sem=ex_send.at[i, d - 1], recv_sem=ex_recv.at[i, d - 1],
                    device_id=peer, device_id_type=MESH,
                )
            )
    local = [
        pltpu.make_async_copy(suf_hbm, suf_g.at[me], ex_local.at[0]),
        pltpu.make_async_copy(new_src, new_g.at[me], ex_local.at[1]),
    ]
    for c in exchange + local:
        c.start()

    for c in small[:2]:
        c.wait()
    key = iota((n_ext, particles), 0)
    col = iota((n_ext, particles), 1)
    suf_particle = key >> log2_int(suf_dev)
    suf_pos = (key & (suf_dev - 1)) + z * suf_dev
    reach = (key < n_suf) & (suf_particle == col) & (suf_pos < len_ref[...])
    state = jnp.where(reach, 1.0, 0.0)
    rest = key - n_suf
    new_particle = (rest >> log2_int(chunk)) * per + (rest & (chunk - 1)) + p0
    is_new = jnp.where(
        (rest >= 0) & (rest < n_new) & (new_particle == col), 1.0, 0.0
    )
    spread = jnp.where(
        iota((width, particles), 1) == (iota((width, particles), 0) >> log2_int(group)) + me * per,
        1.0, 0.0,
    ).astype(BF16)
    for s in range(steps):
        parents = anc_ref[pl.ds(s, 1), :]
        move = jnp.where(iota((particles, particles), 0) == parents, 1.0, 0.0).astype(BF16)
        state = nn(state.astype(BF16), move)
        state = state + is_new * jnp.where(my_step == s, 1.0, 0.0)
        mask[s] = jnp.where(nt(spread, state.astype(BF16)) > 0.5, 0.0, MASKED)

    size = 1024
    for src, dst in ((0, kf), (1, vf)):
        for j in range(PIECES):
            loads[src][j].wait()

            def widen(i, _, src=src, dst=dst, j=j):
                at = pl.ds(pl.multiple_of(j * piece + i * size, size), size)
                dst[at, :] = raw[src, at, :].astype(F32)
                return 0

            lax.fori_loop(0, piece // size, widen, 0)

    small[2].wait()
    eye = iota((width, width), 0) == iota((width, width), 1)

    def parts(b):
        h = b // groups_of_steps
        return h, (b - h * groups_of_steps) * SG

    def to_lanes(x):
        return jnp.sum(jnp.where(eye, x, 0.0), axis=0, keepdims=True)

    def to_rows(x):
        return jnp.sum(jnp.where(eye, jnp.broadcast_to(x, eye.shape), 0.0), axis=1, keepdims=True)

    def head_tile(ref, h, i):
        return ref[pl.ds(h + i * TILE * heads, TILE, stride=heads), :].astype(BF16)

    def attend(b, use_prompt, use_extra):
        h, s0 = parts(b)
        q = jnp.concatenate(
            [q_ref[s0 + i, :, h].astype(F32).reshape(width, hd) for i in range(SG)], axis=0
        ).astype(BF16)
        tiles = []
        if use_prompt:
            for i in range(prompt // TILE):
                tiles.append((
                    i * TILE, TILE, None,
                    lambda i=i: head_tile(kf, h, i), lambda i=i: head_tile(vf, h, i),
                ))
        if use_extra:
            tiles.append((
                prompt, n_ext,
                lambda: jnp.concatenate([mask[s0 + i] for i in range(SG)], axis=0),
                lambda: kx[h], lambda: vx[h],
            ))
        peak = None
        for at, size, bias, keys, _ in tiles:
            score = nt(q, keys())
            if bias is not None:
                score = score + bias()
            s_scr[:, pl.ds(at, size)] = score
            for i in range(0, size, hd):
                part = score[:, i:i + hd]
                peak = part if peak is None else jnp.maximum(peak, part)
        peak = jnp.max(peak, axis=1, keepdims=True)
        sums = [None, None]
        for n, (at, size, _, _, values) in enumerate(tiles):
            w = jnp.exp2((s_scr[:, pl.ds(at, size)] - peak) * score_mul).astype(BF16)
            v = values()
            part = nn(w, jnp.concatenate([v, jnp.ones_like(v)], axis=1))
            sums[n % 2] = part if sums[n % 2] is None else sums[n % 2] + part
        both = sums[0]
        if sums[1] is not None:
            half_scr[...] = sums[1]
            both = both + half_scr[...]
        total = both[:, hd:]
        return both[:, :hd] / total, peak * score_mul + jnp.log2(total)

    def put(b, out, lse):
        for i in range(SG):
            c = b * SG + i
            at = slice(i * width, (i + 1) * width)
            own[c] = out[at]
            stat[c] = to_lanes(lse[at])

            @pl.when(jnp.logical_not(has_outer))
            def _(c=c, at=at):
                msg[c] = out[at].astype(BF16)
                send(c)

    def weight(first, second):
        top = jnp.maximum(first, second)
        e1, e2 = jnp.exp2(first - top), jnp.exp2(second - top)
        return e1 / (e1 + e2), top + jnp.log2(e1 + e2)

    def unpack_extra():
        for c in local:
            c.wait()
        for c in exchange:
            c.wait()
        ps, pn = suf_g.shape[2], new_g.shape[2]
        for o in range(owners):
            for i, dst in enumerate((sfk, sfv)):
                dst[pl.ds(o * ps, ps), :] = suf_g[o, i].astype(F32)
            for i, dst in enumerate((nfk, nfv)):
                dst[pl.ds(o * pn, pn), :] = new_g[o, i].astype(F32)
        for h in range(heads):
            for suf, new, dst in ((sfk, nfk, kx), (sfv, nfv, vx)):
                pieces = [
                    suf[pl.ds(h, n_suf, stride=heads), :], new[pl.ds(h, n_new, stride=heads), :]
                ]
                if n_ext > n_suf + n_new:
                    pieces.append(jnp.zeros((n_ext - n_suf - n_new, hd), F32))
                dst[h] = jnp.concatenate(pieces, axis=0).astype(BF16)

    mid = (z == lo) | (z == hi)
    left_half = z <= lo
    inner = jnp.where(left_half, z + 1, z - 1)
    outer = jnp.where(left_half, z - 1, z + 1)
    has_outer = (z > 0) & (z < n_ctx - 1)

    def inward(c, across):
        data, small_to, sems = (
            (got_in, gst_in, rs_recv_in) if across else (got_out, gst_out, rs_recv_out)
        )
        return [
            pltpu.make_async_remote_copy(
                src_ref=src.at[c], dst_ref=dst.at[c],
                send_sem=rs_send.at[i, c], recv_sem=sems.at[i, c],
                device_id={"ctx": inner}, device_id_type=MESH,
            )
            for i, (src, dst) in enumerate(((stat, small_to), (msg, data)))
        ]

    def place(c):
        h = c // steps
        return out_ref.at[c - h * steps, :, h]

    def outward(c):
        return pltpu.make_async_remote_copy(
            src_ref=place(c), dst_ref=place(c),
            send_sem=ag_send.at[c], recv_sem=ag_recv.at[c],
            device_id={"ctx": outer}, device_id_type=MESH,
        )

    def send(c):
        for across in (True, False):
            @pl.when(mid if across else jnp.logical_not(mid))
            def _(across=across):
                for copy in inward(c, across):
                    copy.start()

    def fold_stage(c):
        for copy in inward(c, False):
            copy.wait_recv()
        share, lse = weight(stat[c], gst_out[c])
        theirs = got_out[c].astype(F32)
        msg[c] = (theirs + to_rows(share) * (own[c] - theirs)).astype(BF16)
        stat[c] = lse
        send(c)

    def swap_stage(c):
        for copy in inward(c, True):
            copy.wait_recv()
        mine, theirs = (stat[c], msg[c].astype(F32)), (gst_in[c], got_in[c].astype(F32))
        low = [jnp.where(left_half, a, b) for a, b in zip(mine, theirs)]
        high = [jnp.where(left_half, b, a) for a, b in zip(mine, theirs)]
        share, _ = weight(low[0], high[0])
        done = high[1] + to_rows(share) * (low[1] - high[1])
        place(c)[...] = done.reshape(per, group, hd).astype(BF16)

        @pl.when(has_outer)
        def _():
            outward(c).start()

    def each(stage, b):
        for i in range(SG):
            stage(b * SG + i)

    out, lse = attend(0, True, False)
    own[pl.ds(0, SG)] = out.reshape(SG, width, hd)
    lse_scr[...] = lse
    unpack_extra()
    out_x, lse_x = attend(0, False, True)
    share, lse = weight(lse_scr[...], lse_x)
    put(0, out_x + share * (own[pl.ds(0, SG)].reshape(rows, hd) - out_x), lse)

    fold_delay = jnp.where(left_half, FOLD_LEFT, FOLD_RIGHT)
    swap_delay = jnp.where(left_half, SWAP_LEFT, SWAP_RIGHT)

    def run(i, _):
        @pl.when(i < nb)
        def _():
            put(i, *attend(i, True, True))

        for on, delay, stage in ((has_outer, fold_delay, fold_stage), (mid, swap_delay, swap_stage)):
            @pl.when(on & (i >= delay) & (i < nb + delay))
            def _(delay=delay, stage=stage):
                each(stage, i - delay)
        return 0

    lax.fori_loop(1, nb + max(FOLD_LEFT, FOLD_RIGHT, SWAP_LEFT, SWAP_RIGHT), run, 0)

    def close(c, _):
        @pl.when(jnp.logical_not(mid))
        def _():
            outward(c).wait_recv()

            @pl.when(has_outer)
            def _():
                outward(c).start()

        for across in (True, False):
            @pl.when(mid if across else jnp.logical_not(mid))
            def _(across=across):
                for copy in inward(c, across):
                    copy.wait_send()

        @pl.when(has_outer)
        def _():
            outward(c).wait_send()
        return 0

    lax.fori_loop(0, nb * SG, close, 0)


def on_device(n_ctx, owners, queries, prompt_cache, suffix_cache, new_kv, ancestors, lengths):
    steps, per, heads, group, hd = queries.shape
    prompt = prompt_cache.shape[1]
    suf_dev = suffix_cache.shape[2]
    particles = ancestors.shape[1]
    width = per * group
    rows = SG * width
    nc = heads * steps
    shares = n_ctx // steps
    chunk = per // shares
    n_ext = -(-(particles * suf_dev + owners * chunk) // 128) * 128
    dma = pltpu.SemaphoreType.DMA
    score_mul = math.log2(math.e) / math.sqrt(hd)
    ps, pn = per * suf_dev * heads, chunk * heads
    any_spec = pl.BlockSpec(memory_space=pl.ANY)
    vmem_spec = pl.BlockSpec(memory_space=pltpu.VMEM)
    return pl.pallas_call(
        functools.partial(kernel, n_ctx, owners, suf_dev, score_mul),
        out_shape=pltpu.VMEM(queries.shape, BF16),
        in_specs=[any_spec] * 6,
        out_specs=vmem_spec,
        scratch_shapes=[
            pltpu.VMEM(queries.shape, BF16),
            pltpu.VMEM(ancestors.shape, jnp.int32),
            pltpu.VMEM((1, particles), jnp.int32),
            pltpu.VMEM((2, prompt * heads, hd), BF16),
            pltpu.VMEM((prompt * heads, hd), F32),
            pltpu.VMEM((prompt * heads, hd), F32),
            pltpu.VMEM((heads, n_ext, hd), BF16),
            pltpu.VMEM((heads, n_ext, hd), BF16),
            pltpu.VMEM((rows, prompt + n_ext), F32),
            pltpu.VMEM((rows, hd), F32),
            pltpu.VMEM((rows, 2 * hd), F32),
            pltpu.VMEM((owners, 2, ps, hd), BF16),
            pltpu.VMEM((owners, 2, pn, hd), BF16),
            pltpu.VMEM((owners * ps, hd), F32),
            pltpu.VMEM((owners * ps, hd), F32),
            pltpu.VMEM((owners * pn, hd), F32),
            pltpu.VMEM((owners * pn, hd), F32),
            pltpu.VMEM((steps, width, n_ext), F32),
            pltpu.VMEM((nc, width, hd), F32),
            pltpu.VMEM((nc, 1, width), F32),
            pltpu.VMEM((nc, width, hd), BF16),
            pltpu.VMEM((nc, width, hd), BF16),
            pltpu.VMEM((nc, width, hd), BF16),
            pltpu.VMEM((nc, 1, width), F32),
            pltpu.VMEM((nc, 1, width), F32),
            dma((2, PIECES)),
            dma((3,)),
            dma((2,)),
            dma((2, max(owners - 1, 1))),
            dma((2, max(owners - 1, 1))),
            dma((2, nc)),
            dma((2, nc)),
            dma((2, nc)),
            dma((nc,)),
            dma((nc,)),
        ],
        compiler_params=pltpu.CompilerParams(
            collective_id=0, has_side_effects=True, vmem_limit_bytes=58 << 20
        ),
    )(
        queries,
        prompt_cache.reshape(2, prompt * heads, hd),
        suffix_cache.reshape(2, ps, hd),
        new_kv.reshape(steps, 2, per * heads, hd),
        ancestors,
        lengths.reshape(1, particles),
    )


def solution(mesh):
    return jax.shard_map(
        functools.partial(on_device, mesh.shape["ctx"], mesh.shape["dom"]),
        mesh=mesh,
        in_specs=(
            P("groups", "dom", "tp", None, None),
            P("groups", "ctx", "tp", None),
            P("groups", "dom", "ctx", "tp", None),
            P("groups", None, "dom", "tp", None),
            P("groups", None),
            P("groups"),
        ),
        out_specs=P("groups", "dom", "tp", None, None),
        check_vma=False,
    )
```
